32 devices in a mesh: wshard: 4 (over y, x), ctx: 2 (over core), tp: 4 (over z).
Axes of the slice: x: 2, y: 2, z: 4, core: 2. Of those that a mesh axis runs over, the one named last changes fastest.
Arguments:
- tokens: bfloat16 [4, 2048, 768], P('wshard', 'ctx'), may hold values from -6 to 6
- lengths: int32 [4], P('wshard'), may hold values from 512 to 2048, as said below
- qkv_weight: bfloat16 [768, 3, 768], P('wshard', None, 'tp'), may hold values from -0.21875 to 0.21875
- qv_bias: float32 [2, 768], P(None, 'tp'), may hold values from -3 to 3
- out_weight: bfloat16 [768, 768], P('wshard', 'tp'), may hold values from -0.75 to 0.75
- out_bias: float32 [768], replicated, may hold values from -3 to 3
- ln1_gain: float32 [768], replicated, may hold values from 0.5 to 1.5
- ln1_bias: float32 [768], replicated, may hold values from -3 to 3
- gated_weight: bfloat16 [768, 2, 3072], P('wshard', None, 'tp'), may hold values from -0.21875 to 0.21875
- down_weight: bfloat16 [768, 3072], P('wshard', 'tp'), may hold values from -0.109375 to 0.109375
- down_bias: float32 [768], replicated, may hold values from -3 to 3
- ln2_gain: float32 [768], replicated, may hold values from 0.5 to 1.5
- ln2_bias: float32 [768], replicated, may hold values from -3 to 3
- cotangent: bfloat16 [4, 2048, 768], P('wshard', 'ctx'), may hold values from -6 to 6
Outputs:
- layer_output: bfloat16 [4, 2048, 768], P('wshard', 'ctx')
- input_grad: float32 [4, 2048, 768], P('wshard', 'ctx')
- qkv_grad: float32 [768, 3, 768], P('wshard', None, 'tp')
- qvbias_grad: float32 [2, 768], P(None, 'tp')
- outw_grad: float32 [768, 768], P('wshard', 'tp')
- outb_grad: float32 [768], replicated
- ln1g_grad: float32 [768], replicated
- ln1b_grad: float32 [768], replicated
- gated_grad: float32 [768, 2, 3072], P('wshard', None, 'tp')
- down_grad: float32 [768, 3072], P('wshard', 'tp')
- downb_grad: float32 [768], replicated
- ln2g_grad: float32 [768], replicated
- ln2b_grad: float32 [768], replicated
The draws below stay inside these ranges and needn't reach their ends.
Inputs may be any that keep to these rules, and one draw needn't show every extreme that they name: Each sequence holds lengths[s] valid positions at its start; in every draw some sequence is full (2048) and some has exactly 512.
All inputs are finite; a program needn't handle non-finite values.
Results may differ from the reference program's by a relative error of at most 0.014.
The reference program's roundings to bfloat16 on the way count: a program that leaves them out, or rounds other values in their place, can miss the bound.
Values may be sent and summed in bfloat16 or wider, within the bound.
No kernel may reach another device: no remote copies, remote signals or barrier semaphores. Data moves between devices by JAX's collectives and lax.ppermute only.
A program may use at most 128 MiB of HBM per device.

```python
import jax
import jax.numpy as jnp
from jax import lax

D = 768
HEADS = 12
DH = 64
FF = 3072
LEN = 2048
SEQS = 4


def draw_lengths(key, part):
    drawn = jax.random.randint(jax.random.fold_in(key, 1), (SEQS,), LEN // 4, LEN + 1)
    first_pick = jax.random.randint(jax.random.fold_in(key, 2), (), 0, SEQS)
    offset = jax.random.randint(jax.random.fold_in(key, 3), (), 1, SEQS)
    second_pick = (first_pick + offset) % SEQS
    places = jnp.arange(SEQS)
    drawn = jnp.where(places == first_pick, LEN, drawn)
    drawn = jnp.where(places == second_pick, LEN // 4, drawn)
    return drawn.astype(jnp.int32)


def strengthened(values, stream_key, source, target, shards_of, factor):
    owner, partner = [(jnp.arange(values.shape[dim]) // (values.shape[dim] // shards_of)).reshape([-1 if axis == dim else 1 for axis in range(values.ndim)]) for dim in (source, target)]
    chosen = jax.random.permutation(stream_key, shards_of)[partner]
    strong = (owner == chosen) | (owner == (partner + shards_of // 2) % shards_of)
    return jnp.where(strong, factor * values, values)


def level_of(key, dims, pieces, smallest, largest):
    gain = 1.0
    for axis_at, blocks in pieces:
        heights = jax.random.uniform(jax.random.fold_in(jax.random.fold_in(key, 6), axis_at), (blocks,), jnp.float32, smallest / len(pieces), largest / len(pieces))
        gain = gain * jnp.repeat(jnp.exp(heights), dims[axis_at] // blocks).reshape((-1,) + (1,) * (len(dims) - 1 - axis_at))
    return gain


def centred(key, extent, width, most, pieces=(), held_as=jnp.bfloat16):
    array = width * jax.random.normal(key, extent, jnp.float32)
    if pieces:
        array = array * level_of(key, extent, pieces, -0.22, 0.18)
    return jnp.clip(array, -most, most).astype(held_as)


def bell_draw_with(key, dims, scale, bound, pieces, heavy, held_as=jnp.bfloat16):
    result = scale * jax.random.normal(key, dims, jnp.float32)
    if pieces:
        result = result * level_of(key, dims, pieces, -0.22, 0.18)
    return jnp.clip(strengthened(result, jax.random.fold_in(key, 3), *heavy), -bound, bound).astype(held_as)


def setup_inputs(seed: int = 0) -> dict:
    streams_of = jax.random.split(jax.random.key(seed), 15)
    return {
        "tokens": bell_draw_with(streams_of[0], (SEQS, LEN, D), 1.0, 6.0, ((0, 4), (1, 2)), (0, 2, 4, 2.0)),
        "lengths": draw_lengths(jax.random.fold_in(streams_of[14], 71), 0),
        "qkv_weight": centred(streams_of[2], (D, 3, D), D ** -0.5, 0.21875, ((0, 4), (2, 4))),
        "qv_bias": centred(streams_of[3], (2, D), 0.5, 3.0, ((1, 4),), jnp.float32),
        "out_weight": centred(streams_of[4], (D, D), DH ** -0.5, 0.75, ((0, 4), (1, 4))),
        "out_bias": centred(streams_of[5], (D,), 0.5, 3.0, (), jnp.float32),
        "ln1_gain": jnp.clip(1.0 + 0.1 * jax.random.normal(streams_of[6], (D,), jnp.float32), 0.5, 1.5),
        "ln1_bias": centred(streams_of[7], (D,), 0.5, 3.0, (), jnp.float32),
        "gated_weight": centred(streams_of[8], (D, 2, FF), D ** -0.5, 0.21875, ((0, 4), (2, 4))),
        "down_weight": centred(streams_of[9], (D, FF), FF ** -0.5, 0.109375, ((0, 4), (1, 4))),
        "down_bias": centred(streams_of[10], (D,), 0.5, 3.0, (), jnp.float32),
        "ln2_gain": jnp.clip(1.0 + 0.1 * jax.random.normal(streams_of[11], (D,), jnp.float32), 0.5, 1.5),
        "ln2_bias": centred(streams_of[12], (D,), 0.5, 3.0, (), jnp.float32),
        "cotangent": bell_draw_with(streams_of[13], (SEQS, LEN, D), 1.0, 6.0, ((0, 4), (1, 2)), (0, 2, 4, 2.0)),
    }


@jax.custom_vjp
def low(v):
    return lax.optimization_barrier(v.astype(jnp.bfloat16)).astype(jnp.float32)

@jax.custom_vjp
def low_back(v):
    return v

def low_keep(v):
    return (low(v), None)

def low_pass(kept, grad):
    return (grad,)

def back_keep(v):
    return (v, None)

def back_low(kept, grad):
    return (low(grad),)
low.defvjp(low_keep, low_pass)
low_back.defvjp(back_keep, back_low)
norm_eps = 1e-05
highest = lax.Precision.HIGHEST

def layer_norm(inputs, norm_gain, norm_shift):
    center = inputs - lax.optimization_barrier(jnp.mean(inputs, axis=-1, keepdims=True))
    spread = lax.optimization_barrier(jnp.mean(center * center, axis=-1, keepdims=True))
    return center * lax.rsqrt(spread + norm_eps) * norm_gain + norm_shift

def sequence_forward(params, seq_tokens, length):
    qkv_weight, qv_bias, out_weight, out_bias, ln1_gain, ln1_bias, gated_weight, down_weight, down_bias, ln2_gain, ln2_bias = params
    projected = jnp.einsum('td,dkf->tkf', seq_tokens, qkv_weight, precision=highest)
    queries = low(low_back(projected[:, 0] + qv_bias[0])).reshape(LEN, HEADS, DH)
    key_block = low(low_back(projected[:, 1])).reshape(LEN, HEADS, DH)
    value_block = low(low_back(projected[:, 2] + qv_bias[1])).reshape(LEN, HEADS, DH)
    raw_scores = low_back(jnp.einsum('qhe,khe->hqk', queries, key_block, precision=highest) * DH ** (-0.5))
    position = jnp.arange(LEN, dtype=jnp.int32)
    distance = jnp.abs(position[:, None] - position[None, :]).astype(jnp.float32)
    slopes = 2.0 ** (-8.0 * (jnp.arange(HEADS, dtype=jnp.int32) + 1).astype(jnp.float32) / HEADS)
    biased = raw_scores - slopes[:, None, None] * distance[None, :, :]
    scores = jnp.where((position < length)[None, None, :], biased, -1e+30)
    row_top = lax.optimization_barrier(jnp.max(scores, axis=-1, keepdims=True))
    exponent = jnp.exp(scores - row_top)
    attention = low(exponent / lax.optimization_barrier(jnp.sum(exponent, axis=-1, keepdims=True)))
    mixture = jnp.einsum('hqk,khe->qhe', attention, value_block, precision=highest).reshape(LEN, D)
    mixture = low(low_back(mixture))
    pre_first = seq_tokens + low_back(jnp.dot(mixture, out_weight.T, precision=highest)) + out_bias
    norm_first = layer_norm(pre_first, ln1_gain, ln1_bias)
    gate_up = low_back(jnp.einsum('td,dgf->tgf', low(norm_first), gated_weight, precision=highest))
    activation = low(jax.nn.gelu(gate_up[:, 0], approximate=False) * gate_up[:, 1])
    pre_second = norm_first + low_back(jnp.dot(activation, down_weight.T, precision=highest)) + down_bias
    return layer_norm(pre_second, ln2_gain, ln2_bias)

def reference(tokens, lengths, qkv_weight, qv_bias, out_weight, out_bias, ln1_gain, ln1_bias, gated_weight, down_weight, down_bias, ln2_gain, ln2_bias, cotangent):
    params = (qkv_weight.astype(jnp.float32), qv_bias.astype(jnp.float32), out_weight.astype(jnp.float32), out_bias.astype(jnp.float32), ln1_gain.astype(jnp.float32), ln1_bias.astype(jnp.float32), gated_weight.astype(jnp.float32), down_weight.astype(jnp.float32), down_bias.astype(jnp.float32), ln2_gain.astype(jnp.float32), ln2_bias.astype(jnp.float32))
    seq_inputs = tokens.astype(jnp.float32)

    def whole(weights, inputs):

        def one_sequence(carry, entry):
            return (carry, jax.checkpoint(sequence_forward)(weights, entry[0], entry[1]))
        unused, results = lax.scan(one_sequence, jnp.zeros((), jnp.float32), (inputs, lengths))
        return results
    layer_values, pull = jax.vjp(whole, params, seq_inputs)
    weight_grads, input_grad = pull(cotangent.astype(jnp.float32))
    return (layer_values.astype(jnp.bfloat16), input_grad, weight_grads[0], weight_grads[1], weight_grads[2], weight_grads[3], weight_grads[4], weight_grads[5], weight_grads[6], weight_grads[7], weight_grads[8], weight_grads[9], weight_grads[10])
```

```python
import jax
import jax.numpy as jnp
from jax import lax
from jax.sharding import PartitionSpec as P

HEADS = 12
DH = 64
SCALE = DH ** (-0.5)
norm_eps = 1e-05
f32 = jnp.float32
bf16 = jnp.bfloat16


def layer_norm(inputs, norm_gain, norm_shift):
    center = inputs - jnp.mean(inputs, axis=-1, keepdims=True)
    spread = jnp.mean(center * center, axis=-1, keepdims=True)
    return center * lax.rsqrt(spread + norm_eps) * norm_gain + norm_shift


def gated_unit(gate_part, up_part):
    return jax.nn.gelu(gate_part, approximate=False) * up_part


def mm(left, right):
    return lax.dot_general(left, right, (((1,), (0,)), ((), ())), preferred_element_type=f32)


def mm_nt(left, right):
    return lax.dot_general(left, right, (((1,), (1,)), ((), ())), preferred_element_type=f32)


def mm_tn(left, right):
    return lax.dot_general(left, right, (((0,), (0,)), ((), ())), preferred_element_type=f32)


def log2_of(n):
    if n & (n - 1):
        raise ValueError("axis size")
    return n.bit_length() - 1


def swap(x, axis, mask, n):
    return lax.ppermute(x, axis, [(i, i ^ mask) for i in range(n)])


def pick(stacked, index):
    return lax.dynamic_index_in_dim(stacked, index, 0, keepdims=False)


def gather_wshard(piece, n_ws, n_ctx):
    stages = log2_of(n_ws)
    me, core = lax.axis_index("wshard"), lax.axis_index("ctx")
    held, masks = [piece], [[0] for _ in range(n_ctx)]
    for stage in range(stages):
        bit = [1 << ((stage + c) % stages) for c in range(n_ctx)]
        perm = [
            (w * n_ctx + c, (w ^ bit[c]) * n_ctx + c) for w in range(n_ws) for c in range(n_ctx)
        ]
        sent = held[0][None] if len(held) == 1 else jnp.stack(held)
        got = lax.ppermute(sent, ("wshard", "ctx"), perm)
        held = held + [got[i] for i in range(len(held))]
        masks = [m + [v ^ bit[c] for v in m] for c, m in enumerate(masks)]
    table = jnp.asarray(masks, jnp.int32)
    out = jnp.zeros((n_ws,) + piece.shape, piece.dtype)
    for p, part in enumerate(held):
        out = lax.dynamic_update_index_in_dim(out, part, me ^ table[core, p], 0)
    return out


def sum_all(x, mesh_shape):
    for axis in ("ctx", "tp", "wshard"):
        n = mesh_shape[axis]
        for stage in range(log2_of(n)):
            x = x + swap(x, axis, 1 << stage, n)
    return x


def tp_gather(x, t):
    far = swap(x, "tp", 2, 4)
    high = t // 2
    two = jnp.stack([jnp.where(high == 0, x, far), jnp.where(high == 0, far, x)])
    near = swap(two, "tp", 1, 4)
    low = t % 2
    both = jnp.stack([jnp.where(low == 0, two, near), jnp.where(low == 0, near, two)], axis=1)
    return both.reshape(4 * x.shape[0], x.shape[1])


def tp_scatter(x, t):
    rows, width = x.shape
    parts = x.reshape(2, 2, rows // 4, width)
    high, low = t // 2, t % 2
    away = lax.dynamic_index_in_dim(parts, 1 - low, 1, keepdims=False)
    home = lax.dynamic_index_in_dim(parts, low, 1, keepdims=False)
    home = home + swap(away.astype(bf16), "tp", 1, 4).astype(f32)
    far = pick(home, 1 - high)
    near = pick(home, high)
    return near + swap(far.astype(bf16), "tp", 2, 4).astype(f32)


def make_local(mesh):
    shape = mesh.shape
    n_ws, n_ctx, n_tp = shape["wshard"], shape["ctx"], shape["tp"]
    if n_tp != 4 or n_ctx != 2:
        raise ValueError("mesh")

    def local(
        tokens,
        lengths,
        qkv_weight,
        qv_bias,
        out_weight,
        out_bias,
        ln1_gain,
        ln1_bias,
        gated_weight,
        down_weight,
        down_bias,
        ln2_gain,
        ln2_bias,
        cotangent,
    ):
        seq_dev, length_here, width = tokens.shape
        if seq_dev != 1:
            raise ValueError("one sequence")
        part = qv_bias.shape[1]
        heads = part // DH
        rows = length_here // n_tp
        shard_rows = qkv_weight.shape[0]
        half_rows = shard_rows // n_ctx
        w, c, t = lax.axis_index("wshard"), lax.axis_index("ctx"), lax.axis_index("tp")
        x = tokens[0]
        length = lengths[0]
        head_number = t * heads + jnp.arange(heads, dtype=jnp.int32) + 1
        slopes = 2.0 ** (-8.0 * head_number.astype(f32) / HEADS)

        x_other = swap(x, "ctx", 1, n_ctx)
        qkv = gather_wshard(jnp.transpose(qkv_weight, (1, 0, 2)), n_ws, n_ctx)
        qkv = jnp.transpose(qkv, (1, 0, 2, 3)).reshape(3, width, part)

        out_blocks = lax.all_gather(out_weight, ("wshard", "tp"), axis=0, tiled=False)
        full_out = jnp.transpose(
            out_blocks.reshape(n_ws, n_tp, shard_rows, part), (0, 2, 1, 3)
        ).reshape(width, n_tp * part)

        def own_half(weight):
            return lax.dynamic_slice_in_dim(weight, c * half_rows, half_rows, 0)

        def gather_half(half):
            return lax.all_gather(half, ("wshard", "ctx"), axis=0, tiled=True)

        gated_half, down_half = own_half(gated_weight), own_half(down_weight)
        gated_far, down_far = swap(gated_half, "tp", 2, n_tp), swap(down_half, "tp", 2, n_tp)
        gated = [gather_half(gated_half), gather_half(gated_far)]
        down = [gather_half(down_half), gather_half(down_far)]

        q = (mm(x, qkv[0]) + qv_bias[0]).astype(bf16)
        keys = jnp.concatenate([mm(x, qkv[1]), mm(x_other, qkv[1])], axis=0).astype(bf16)
        values = (
            jnp.concatenate([mm(x, qkv[2]), mm(x_other, qkv[2])], axis=0) + qv_bias[1]
        ).astype(bf16)
        local_pos = jnp.arange(length_here, dtype=jnp.int32)
        q_pos = c * length_here + local_pos
        k_pos = jnp.concatenate([q_pos, (1 - c) * length_here + local_pos])
        qh = q.reshape(length_here, heads, DH)
        kh = keys.reshape(n_ctx * length_here, heads, DH)
        vh = values.reshape(n_ctx * length_here, heads, DH)

        def scores_of():
            raw = jnp.einsum("qhe,khe->hqk", qh, kh, preferred_element_type=f32) * SCALE
            distance = jnp.abs(q_pos[:, None] - k_pos[None, :]).astype(f32)
            biased = raw - slopes[:, None, None] * distance[None]
            return jnp.where((k_pos < length)[None, None, :], biased, -1e30)

        scores = scores_of()
        row_top = jnp.max(scores, axis=-1, keepdims=True)
        exponent = jnp.exp(scores - row_top)
        row_total = jnp.sum(exponent, axis=-1, keepdims=True)
        probs_low = (exponent / row_total).astype(bf16)
        mixed = jnp.einsum("hqk,khe->qhe", probs_low, vh, preferred_element_type=f32)
        mixed = mixed.astype(bf16).reshape(length_here, part)
        log_total = (row_top + jnp.log(row_total))[:, :, 0]

        mixed_rows = lax.all_to_all(mixed, "tp", 0, 1, tiled=True)
        x_rows = lax.dynamic_slice_in_dim(x, t * rows, rows, 0).astype(f32)
        cot_rows = lax.dynamic_slice_in_dim(cotangent[0], t * rows, rows, 0).astype(f32)
        pre1 = x_rows + (mm_nt(mixed_rows, full_out) + out_bias)
        norm1 = layer_norm(pre1, ln1_gain, ln1_bias)
        norm_low = norm1.astype(bf16)

        def neighbour(v):
            return swap(v, "tp", 1, n_tp)

        def forward(rows_low):
            kept, acts, total = [], [], None
            for g, d in zip(gated, down):
                gate, up = mm(rows_low, g[:, 0]), mm(rows_low, g[:, 1])
                act = gated_unit(gate, up).astype(bf16)
                kept.append((gate, up))
                acts.append(act)
                piece = mm_nt(act, d)
                total = piece if total is None else total + piece
            return kept, acts, total

        norm_near = neighbour(norm_low)
        kept_own, acts_own, down_own = forward(norm_low)
        kept_near, acts_near, down_near = forward(norm_near)
        down_sum = down_own + neighbour(down_near.astype(bf16)).astype(f32)
        pre2 = norm1 + (down_sum + down_bias)
        layer_rows, pull2 = jax.vjp(layer_norm, pre2, ln2_gain, ln2_bias)
        grad_pre2, ln2g, ln2b = pull2(cot_rows)
        output_rows = layer_rows.astype(bf16)
        grad_down = grad_pre2.astype(bf16)
        grad_near = neighbour(grad_down)

        def backward(grad_low, kept):
            pieces, total = [], None
            for g, d, (gate, up) in zip(gated, down, kept):
                grad_act = mm(grad_low, d)
                unused, pull = jax.vjp(gated_unit, gate, up)
                grad_gate, grad_up = pull(grad_act)
                grad_gate, grad_up = grad_gate.astype(bf16), grad_up.astype(bf16)
                pieces.append((grad_gate, grad_up))
                piece = mm_nt(grad_gate, g[:, 0]) + mm_nt(grad_up, g[:, 1])
                total = piece if total is None else total + piece
            return pieces, total

        ggu_own, back_own = backward(grad_down, kept_own)
        ggu_near, back_near = backward(grad_near, kept_near)
        back_got = neighbour(back_near.astype(bf16)).astype(f32)

        norm_both = jnp.concatenate([norm_low, norm_near], axis=0)
        grad_both = jnp.concatenate([grad_down, grad_near], axis=0)

        def reduce_rows(v):
            return lax.psum_scatter(v, ("wshard", "ctx"), scatter_dimension=0, tiled=True)

        ffn_shards = []
        for k in (1, 0):
            gg = jnp.concatenate([ggu_own[k][0], ggu_near[k][0]], axis=0)
            gu = jnp.concatenate([ggu_own[k][1], ggu_near[k][1]], axis=0)
            act = jnp.concatenate([acts_own[k], acts_near[k]], axis=0)
            whole = jnp.concatenate(
                [mm_tn(norm_both, gg), mm_tn(norm_both, gu), mm_tn(grad_both, act)], axis=1
            ).astype(bf16)
            ffn_shards.append(reduce_rows(whole))
        ffn_shard = ffn_shards[1].astype(f32) + swap(ffn_shards[0], "tp", 2, n_tp).astype(f32)

        grad_norm1 = grad_pre2 + (back_own + back_got)
        unused, pull1 = jax.vjp(layer_norm, pre1, ln1_gain, ln1_bias)
        grad_pre1, ln1g, ln1b = pull1(grad_norm1)
        grad_attn = grad_pre1.astype(bf16)
        grad_mixed_rows = mm(grad_attn, full_out).astype(bf16)
        grad_mixed = lax.all_to_all(grad_mixed_rows, "tp", 1, 0, tiled=True)
        outw_part = mm_tn(grad_attn, mixed_rows).astype(bf16)
        layer_output = tp_gather(output_rows, t)

        gh = grad_mixed.reshape(length_here, heads, DH)
        attention = jnp.exp(scores_of() - log_total[:, :, None])
        grad_weights = jnp.einsum("qhe,khe->hqk", gh, vh, preferred_element_type=f32)
        row_dot = jnp.sum(grad_weights * attention, axis=-1, keepdims=True)
        grad_scores = (attention * (grad_weights - row_dot)).astype(bf16)
        grad_q = jnp.einsum("hqk,khe->qhe", grad_scores, kh, preferred_element_type=f32) * SCALE
        grad_k = jnp.einsum("hqk,qhe->khe", grad_scores, qh, preferred_element_type=f32) * SCALE
        grad_v = jnp.einsum(
            "hqk,qhe->khe", attention.astype(bf16), gh, preferred_element_type=f32
        )
        grad_q = grad_q.astype(bf16).reshape(length_here, part)
        grad_kv = jnp.concatenate(
            [grad_k.reshape(-1, part), grad_v.reshape(-1, part)], axis=1
        )
        grad_kv = grad_kv[:length_here] + swap(grad_kv[length_here:], "ctx", 1, n_ctx)
        grad_kv = grad_kv.astype(bf16)
        grad_k, grad_v = grad_kv[:, :part], grad_kv[:, part:]

        input_part = mm_nt(grad_q, qkv[0]) + mm_nt(grad_k, qkv[1]) + mm_nt(grad_v, qkv[2])
        input_rows = grad_pre1 + tp_scatter(input_part, t)
        input_grad = tp_gather(input_rows.astype(bf16), t).astype(f32)

        grad_proj = jnp.concatenate([grad_q, grad_k, grad_v], axis=1)
        qkv_out = jnp.concatenate([mm_tn(x, grad_proj).astype(bf16), outw_part], axis=1)
        qkv_out = reduce_rows(qkv_out).astype(f32)
        qkv_shard, outw_shard = qkv_out[:, : 3 * part], qkv_out[:, 3 * part :]
        outw_shard = lax.psum_scatter(outw_shard, "tp", scatter_dimension=1, tiled=True)

        shard = jnp.concatenate([ffn_shard, qkv_shard, outw_shard], axis=1)
        other = swap(shard, "ctx", 1, n_ctx)
        shard = jnp.concatenate(
            [jnp.where(c == 0, shard, other), jnp.where(c == 0, other, shard)], axis=0
        )
        hidden = gated_weight.shape[2]
        gated_grad = shard[:, : 2 * hidden].reshape(shard_rows, 2, hidden)
        down_grad = shard[:, 2 * hidden : 3 * hidden]
        qkv_grad = shard[:, 3 * hidden : 3 * hidden + 3 * part].reshape(shard_rows, 3, part)
        outw_grad = shard[:, 3 * hidden + 3 * part :]

        bias_here = jnp.stack(
            [jnp.sum(grad_q.astype(f32), axis=0), jnp.sum(grad_v.astype(f32), axis=0)]
        )
        bias_slot = lax.dynamic_update_slice_in_dim(
            jnp.zeros((2, width), f32), bias_here, t * part, 1
        )
        sums = jnp.concatenate(
            [
                bias_slot,
                jnp.stack(
                    [jnp.sum(grad_pre1, axis=0), ln1g, ln1b, jnp.sum(grad_pre2, axis=0), ln2g, ln2b]
                ),
            ],
            axis=0,
        )
        sums = sum_all(sums, shape)
        qvbias_grad = lax.dynamic_slice_in_dim(sums[:2], t * part, part, 1)
        return (
            layer_output[None],
            input_grad[None],
            qkv_grad,
            qvbias_grad,
            outw_grad,
            sums[2],
            sums[3],
            sums[4],
            gated_grad,
            down_grad,
            sums[5],
            sums[6],
            sums[7],
        )

    return local


def solution(mesh):
    return jax.shard_map(
        make_local(mesh),
        mesh=mesh,
        in_specs=(
            P("wshard", "ctx", None),
            P("wshard"),
            P("wshard", None, "tp"),
            P(None, "tp"),
            P("wshard", "tp"),
            P(),
            P(),
            P(),
            P("wshard", None, "tp"),
            P("wshard", "tp"),
            P(),
            P(),
            P(),
            P("wshard", "ctx", None),
        ),
        out_specs=(
            P("wshard", "ctx", None),
            P("wshard", "ctx", None),
            P("wshard", None, "tp"),
            P(None, "tp"),
            P("wshard", "tp"),
            P(),
            P(),
            P(),
            P("wshard", None, "tp"),
            P("wshard", "tp"),
            P(),
            P(),
            P(),
        ),
        check_vma=False,
    )
```

```python
import functools

import jax
import jax.numpy as jnp
from jax import lax
from jax.experimental import pallas as pl
from jax.experimental.pallas import tpu as pltpu
from jax.sharding import PartitionSpec as P

HEADS = 12
DH = 64
SCALE = DH ** (-0.5)
norm_eps = 1e-05
f32 = jnp.float32
bf16 = jnp.bfloat16
FAR = 1e32


def layer_norm(inputs, norm_gain, norm_shift):
    center = inputs - jnp.mean(inputs, axis=-1, keepdims=True)
    spread = jnp.mean(center * center, axis=-1, keepdims=True)
    return center * lax.rsqrt(spread + norm_eps) * norm_gain + norm_shift


def gated_unit(gate_part, up_part):
    return jax.nn.gelu(gate_part, approximate=False) * up_part


def mm(left, right):
    return lax.dot_general(left, right, (((1,), (0,)), ((), ())), preferred_element_type=f32)


def mm_nt(left, right):
    return lax.dot_general(left, right, (((1,), (1,)), ((), ())), preferred_element_type=f32)


def mm_tn(left, right):
    return lax.dot_general(left, right, (((0,), (0,)), ((), ())), preferred_element_type=f32)


def head_lanes(x, h):
    lane = lax.broadcasted_iota(jnp.int32, x.shape, 1)
    return jnp.where((lane >= h * DH) & (lane < (h + 1) * DH), x, jnp.zeros_like(x))


def distance_block(ints, start, n_keys, q_start, n_queries, span):
    key = start + lax.broadcasted_iota(jnp.int32, (n_keys, 1), 0)
    own, other = ints[0] * span, (1 - ints[0]) * span
    key = jnp.where(key < span, key + own, key - span + other)
    query = q_start + own + lax.broadcasted_iota(jnp.int32, (1, n_queries), 1)
    valid = key < ints[1]
    key_f = jnp.where(valid, key.astype(f32), FAR)
    return jnp.abs(key_f - query.astype(f32))


def attend_kernel(ints, slopes, q_ref, k_ref, vt_ref, o_ref, lse_ref, *, heads, chunk, span):
    block = q_ref.shape[0]
    q_start = pl.program_id(0) * block
    q = q_ref[...] * SCALE
    masked = [head_lanes(q, h) for h in range(heads)]

    def step(i, carry):
        start = pl.multiple_of(i * chunk, chunk)
        distance = distance_block(ints, start, chunk, q_start, block, span)
        keys = k_ref[pl.ds(start, chunk), :]
        out = []
        for h in range(heads):
            top, total, acc = carry[h]
            s = mm_nt(keys, masked[h]) - slopes[h] * distance
            new_top = jnp.maximum(top, jnp.max(s, axis=0, keepdims=True))
            p = jnp.exp(s - new_top)
            fade = jnp.exp(top - new_top)
            total = total * fade + jnp.sum(p, axis=0, keepdims=True)
            vt = vt_ref[h * DH : (h + 1) * DH, pl.ds(start, chunk)]
            acc = acc * fade + mm(vt, p.astype(bf16))
            out.append((new_top, total, acc))
        return tuple(out)

    init = tuple(
        (
            jnp.full((1, block), -3e38, f32),
            jnp.zeros((1, block), f32),
            jnp.zeros((DH, block), f32),
        )
        for _ in range(heads)
    )
    done = lax.fori_loop(0, k_ref.shape[0] // chunk, step, init)
    acc = jnp.concatenate([a / l for _, l, a in done], axis=0)
    o_ref[...] = acc.T.astype(bf16)
    lse = jnp.concatenate([m + jnp.log(l) for m, l, _ in done], axis=0)
    pad = lse_ref.shape[0] - heads
    lse_ref[...] = jnp.concatenate([lse, jnp.zeros((pad, block), f32)], axis=0)


def attend_back_kernel(
    ints, slopes, q_ref, k_ref, v_ref, kt_ref, lse_ref, o_ref, g_ref, dq_ref, dkv_ref, dqt,
    *, heads, chunk, span
):
    block = q_ref.shape[0]
    q_start = pl.program_id(0) * block
    q = q_ref[...] * SCALE
    g = g_ref[...]
    q_of = [head_lanes(q, h) for h in range(heads)]
    g_of = [head_lanes(g, h) for h in range(heads)]
    weighted = (g.astype(f32) * o_ref[...].astype(f32)).T
    row_dot = [
        jnp.sum(weighted[h * DH : (h + 1) * DH], axis=0, keepdims=True) for h in range(heads)
    ]
    lse = [lse_ref[h : h + 1, :] for h in range(heads)]
    q_all = jnp.concatenate(q_of, axis=0)
    g_all = jnp.concatenate(g_of, axis=0)
    dqt[...] = jnp.zeros_like(dqt)

    @pl.when(pl.program_id(0) == 0)
    def _():
        dkv_ref[...] = jnp.zeros_like(dkv_ref)

    per_half = span // chunk

    def step(i, carry):
        start = pl.multiple_of(i * chunk, chunk)
        distance = distance_block(ints, start, chunk, q_start, block, span)
        keys = k_ref[pl.ds(start, chunk), :]
        values = v_ref[pl.ds(start, chunk), :]
        probs, grads = [], []
        for h in range(heads):
            s = mm_nt(keys, q_of[h]) - slopes[h] * distance
            p = jnp.exp(s - lse[h])
            gp = mm_nt(values, g_of[h])
            ds = (p * (gp - row_dot[h])).astype(bf16)
            rows = slice(h * DH, (h + 1) * DH)
            dqt[rows, :] += mm(kt_ref[rows, pl.ds(start, chunk)], ds)
            probs.append(p.astype(bf16))
            grads.append(ds)
        half = i // per_half
        at = pl.ds(pl.multiple_of((i % per_half) * chunk, chunk), chunk)
        dkv_ref[half, 0, at, :] += mm(jnp.concatenate(grads, axis=1), q_all)
        dkv_ref[half, 1, at, :] += mm(jnp.concatenate(probs, axis=1), g_all)
        return carry

    lax.fori_loop(0, k_ref.shape[0] // chunk, step, 0)
    dq_ref[...] = (dqt[...] * SCALE).T.astype(bf16)


def attention_forward(ints, slopes, q, k, vt, heads):
    rows, part = q.shape
    keys = k.shape[0]
    block, chunk = min(256, rows), min(512, rows)
    pairs = heads * rows * keys
    return pl.pallas_call(
        functools.partial(attend_kernel, heads=heads, chunk=chunk, span=rows),
        grid_spec=pltpu.PrefetchScalarGridSpec(
            num_scalar_prefetch=2,
            grid=(rows // block,),
            in_specs=[
                pl.BlockSpec((block, part), lambda i, *_: (i, 0)),
                pl.BlockSpec((keys, part), lambda i, *_: (0, 0)),
                pl.BlockSpec((part, keys), lambda i, *_: (0, 0)),
            ],
            out_specs=[
                pl.BlockSpec((block, part), lambda i, *_: (i, 0)),
                pl.BlockSpec((8, block), lambda i, *_: (0, i)),
            ],
        ),
        out_shape=[
            jax.ShapeDtypeStruct((rows, part), bf16),
            jax.ShapeDtypeStruct((8, rows), f32),
        ],
        cost_estimate=pl.CostEstimate(
            flops=8 * pairs * DH, bytes_accessed=4 * keys * part, transcendentals=pairs
        ),
        name="attend",
    )(ints, slopes, q, k, vt)


def attention_backward(ints, slopes, q, k, v, kt, lse, o, g, heads):
    rows, part = q.shape
    keys = k.shape[0]
    block, chunk = min(256, rows), min(512, rows)
    pairs = heads * rows * keys
    row_spec = pl.BlockSpec((block, part), lambda i, *_: (i, 0))
    return pl.pallas_call(
        functools.partial(attend_back_kernel, heads=heads, chunk=chunk, span=rows),
        grid_spec=pltpu.PrefetchScalarGridSpec(
            num_scalar_prefetch=2,
            grid=(rows // block,),
            in_specs=[
                row_spec,
                pl.BlockSpec((keys, part), lambda i, *_: (0, 0)),
                pl.BlockSpec((keys, part), lambda i, *_: (0, 0)),
                pl.BlockSpec((part, keys), lambda i, *_: (0, 0)),
                pl.BlockSpec((8, block), lambda i, *_: (0, i)),
                row_spec,
                row_spec,
            ],
            out_specs=[
                row_spec,
                pl.BlockSpec((keys // rows, 2, rows, part), lambda i, *_: (0, 0, 0, 0)),
            ],
            scratch_shapes=[pltpu.VMEM((part, block), f32)],
        ),
        out_shape=[
            jax.ShapeDtypeStruct((rows, part), bf16),
            jax.ShapeDtypeStruct((keys // rows, 2, rows, part), f32),
        ],
        cost_estimate=pl.CostEstimate(
            flops=30 * pairs * DH, bytes_accessed=16 * keys * part, transcendentals=pairs
        ),
        name="attend_back",
    )(ints, slopes, q, k, v, kt, lse, o, g)


def log2_of(n):
    if n & (n - 1):
        raise ValueError("axis size")
    return n.bit_length() - 1


def swap(x, axis, mask, n):
    return lax.ppermute(x, axis, [(i, i ^ mask) for i in range(n)])


def pick(stacked, index):
    return lax.dynamic_index_in_dim(stacked, index, 0, keepdims=False)


def gather_wshard(piece, n_ws, n_ctx):
    stages = log2_of(n_ws)
    me, core = lax.axis_index("wshard"), lax.axis_index("ctx")
    held, masks = [piece], [[0] for _ in range(n_ctx)]
    for stage in range(stages):
        bit = [1 << ((stage + c) % stages) for c in range(n_ctx)]
        perm = [
            (w * n_ctx + c, (w ^ bit[c]) * n_ctx + c) for w in range(n_ws) for c in range(n_ctx)
        ]
        sent = held[0][None] if len(held) == 1 else jnp.stack(held)
        got = lax.ppermute(sent, ("wshard", "ctx"), perm)
        held = held + [got[i] for i in range(len(held))]
        masks = [m + [v ^ bit[c] for v in m] for c, m in enumerate(masks)]
    table = jnp.asarray(masks, jnp.int32)
    out = jnp.zeros((n_ws,) + piece.shape, piece.dtype)
    for p, part in enumerate(held):
        out = lax.dynamic_update_index_in_dim(out, part, me ^ table[core, p], 0)
    return out


def pair_up(mine, theirs, high):
    return jnp.stack([jnp.where(high == 0, mine, theirs), jnp.where(high == 0, theirs, mine)])


def sum_all(x, mesh_shape):
    for axis in ("ctx", "tp", "wshard"):
        n = mesh_shape[axis]
        for stage in range(log2_of(n)):
            x = x + swap(x, axis, 1 << stage, n)
    return x


def tp_gather(x, t):
    far = swap(x, "tp", 2, 4)
    high = t // 2
    two = jnp.stack([jnp.where(high == 0, x, far), jnp.where(high == 0, far, x)])
    near = swap(two, "tp", 1, 4)
    low = t % 2
    both = jnp.stack([jnp.where(low == 0, two, near), jnp.where(low == 0, near, two)], axis=1)
    return both.reshape(4 * x.shape[0], x.shape[1])


def tp_scatter(x, t):
    rows, width = x.shape
    parts = x.reshape(2, 2, rows // 4, width)
    high, low = t // 2, t % 2
    away = lax.dynamic_index_in_dim(parts, 1 - low, 1, keepdims=False)
    home = lax.dynamic_index_in_dim(parts, low, 1, keepdims=False)
    home = home + swap(away.astype(bf16), "tp", 1, 4).astype(f32)
    far = pick(home, 1 - high)
    near = pick(home, high)
    return near + swap(far.astype(bf16), "tp", 2, 4).astype(f32)


def make_local(mesh):
    shape = mesh.shape
    n_ws, n_ctx, n_tp = shape["wshard"], shape["ctx"], shape["tp"]
    if n_tp != 4 or n_ctx != 2:
        raise ValueError("mesh")

    def local(
        tokens,
        lengths,
        qkv_weight,
        qv_bias,
        out_weight,
        out_bias,
        ln1_gain,
        ln1_bias,
        gated_weight,
        down_weight,
        down_bias,
        ln2_gain,
        ln2_bias,
        cotangent,
    ):
        seq_dev, length_here, width = tokens.shape
        if seq_dev != 1:
            raise ValueError("one sequence")
        part = qv_bias.shape[1]
        heads = part // DH
        rows = length_here // n_tp
        shard_rows = qkv_weight.shape[0]
        half_rows = shard_rows // n_ctx
        w, c, t = lax.axis_index("wshard"), lax.axis_index("ctx"), lax.axis_index("tp")
        x = tokens[0]
        length = lengths[0]
        head_number = t * heads + jnp.arange(heads, dtype=jnp.int32) + 1
        slopes = 2.0 ** (-8.0 * head_number.astype(f32) / HEADS)

        x_other = swap(x, "ctx", 1, n_ctx)
        qkv = gather_wshard(jnp.transpose(qkv_weight, (1, 0, 2)), n_ws, n_ctx)
        qkv = jnp.transpose(qkv, (1, 0, 2, 3)).reshape(3, width, part)

        def own_half(weight):
            return lax.dynamic_slice_in_dim(weight, c * half_rows, half_rows, 1)

        ffn_half = own_half(
            jnp.concatenate([jnp.transpose(gated_weight, (1, 0, 2)), down_weight[None]], axis=0)
        )
        ffn_far = swap(ffn_half, "tp", 2, n_tp)

        def gather_half(half):
            return lax.all_gather(half, ("wshard", "ctx"), axis=1, tiled=True)

        ffn = [gather_half(ffn_half), gather_half(ffn_far)]

        two = pair_up(out_weight, swap(out_weight, "tp", 1, n_tp), t % 2)
        four = pair_up(two, swap(two, "tp", 2, n_tp), t // 2)
        full_out = gather_wshard(four, n_ws, n_ctx)
        full_out = jnp.transpose(
            full_out.reshape(n_ws, n_tp, shard_rows, part), (0, 2, 1, 3)
        ).reshape(width, n_tp * part)

        q = (mm(x, qkv[0]) + qv_bias[0]).astype(bf16)
        keys = jnp.concatenate([mm(x, qkv[1]), mm(x_other, qkv[1])], axis=0).astype(bf16)
        values = (
            jnp.concatenate([mm(x, qkv[2]), mm(x_other, qkv[2])], axis=0) + qv_bias[1]
        ).astype(bf16)
        ints = jnp.stack([c.astype(jnp.int32), length])
        mixed, lse = attention_forward(ints, slopes, q, keys, values.T, heads)

        mixed_rows = lax.all_to_all(mixed, "tp", 0, 1, tiled=True)
        x_rows = lax.dynamic_slice_in_dim(x, t * rows, rows, 0).astype(f32)
        cot_rows = lax.dynamic_slice_in_dim(cotangent[0], t * rows, rows, 0).astype(f32)
        pre1 = x_rows + (mm_nt(mixed_rows, full_out) + out_bias)
        norm1 = layer_norm(pre1, ln1_gain, ln1_bias)
        norm_low = norm1.astype(bf16)

        def neighbour(v):
            return swap(v, "tp", 1, n_tp)

        def forward(rows_low):
            kept, acts, total = [], [], None
            for wts in ffn:
                gate, up = mm(rows_low, wts[0]), mm(rows_low, wts[1])
                act = gated_unit(gate, up).astype(bf16)
                kept.append((gate, up))
                acts.append(act)
                piece = mm_nt(act, wts[2])
                total = piece if total is None else total + piece
            return kept, acts, total

        norm_near = neighbour(norm_low)
        kept_own, acts_own, down_own = forward(norm_low)
        kept_near, acts_near, down_near = forward(norm_near)
        down_sum = down_own + neighbour(down_near.astype(bf16)).astype(f32)
        pre2 = norm1 + (down_sum + down_bias)
        layer_rows, pull2 = jax.vjp(layer_norm, pre2, ln2_gain, ln2_bias)
        grad_pre2, ln2g, ln2b = pull2(cot_rows)
        output_rows = layer_rows.astype(bf16)
        grad_down = grad_pre2.astype(bf16)
        grad_near = neighbour(grad_down)

        def backward(grad_low, kept):
            pieces, total = [], None
            for wts, (gate, up) in zip(ffn, kept):
                grad_act = mm(grad_low, wts[2])
                unused, pull = jax.vjp(gated_unit, gate, up)
                grad_gate, grad_up = pull(grad_act)
                grad_gate, grad_up = grad_gate.astype(bf16), grad_up.astype(bf16)
                pieces.append((grad_gate, grad_up))
                piece = mm_nt(grad_gate, wts[0]) + mm_nt(grad_up, wts[1])
                total = piece if total is None else total + piece
            return pieces, total

        ggu_own, back_own = backward(grad_down, kept_own)
        ggu_near, back_near = backward(grad_near, kept_near)
        back_got = neighbour(back_near.astype(bf16)).astype(f32)

        norm_both = jnp.concatenate([norm_low, norm_near], axis=0)
        grad_both = jnp.concatenate([grad_down, grad_near], axis=0)

        def reduce_rows(v):
            return lax.psum_scatter(v, ("wshard", "ctx"), scatter_dimension=0, tiled=True)

        def ffn_grads(k):
            gg = jnp.concatenate([ggu_own[k][0], ggu_near[k][0]], axis=0)
            gu = jnp.concatenate([ggu_own[k][1], ggu_near[k][1]], axis=0)
            act = jnp.concatenate([acts_own[k], acts_near[k]], axis=0)
            return [
                mm_tn(norm_both, gg).astype(bf16),
                mm_tn(norm_both, gu).astype(bf16),
                mm_tn(grad_both, act).astype(bf16),
            ]

        far_shard = reduce_rows(jnp.concatenate(ffn_grads(1), axis=1))

        grad_norm1 = grad_pre2 + (back_own + back_got)
        unused, pull1 = jax.vjp(layer_norm, pre1, ln1_gain, ln1_bias)
        grad_pre1, ln1g, ln1b = pull1(grad_norm1)
        grad_attn = grad_pre1.astype(bf16)
        grad_mixed_rows = mm(grad_attn, full_out).astype(bf16)
        grad_mixed = lax.all_to_all(grad_mixed_rows, "tp", 1, 0, tiled=True)
        outw_part = mm_tn(grad_attn, mixed_rows).astype(bf16)
        own_shard = reduce_rows(jnp.concatenate(ffn_grads(0) + [outw_part], axis=1))
        hidden = gated_weight.shape[2]
        ffn_shard = own_shard[:, : 3 * hidden].astype(f32) + swap(far_shard, "tp", 2, n_tp).astype(
            f32
        )
        outw_cols = own_shard[:, 3 * hidden :].astype(f32).reshape(half_rows, n_tp, part)
        outw_shard = tp_scatter(
            jnp.transpose(outw_cols, (1, 0, 2)).reshape(n_tp * half_rows, part), t
        )
        layer_output = tp_gather(output_rows, t)

        grad_q, grad_kv = attention_backward(
            ints, slopes, q, keys, values, keys.T, lse, mixed, grad_mixed, heads
        )
        grad_kv = (grad_kv[0] + swap(grad_kv[1], "ctx", 1, n_ctx)).astype(bf16)
        grad_k, grad_v = grad_kv[0], grad_kv[1]

        input_part = mm_nt(grad_q, qkv[0]) + mm_nt(grad_k, qkv[1]) + mm_nt(grad_v, qkv[2])
        input_rows = grad_pre1 + tp_scatter(input_part, t)
        input_grad = tp_gather(input_rows.astype(bf16), t).astype(f32)

        grad_proj = jnp.concatenate([grad_q, grad_k, grad_v], axis=1)
        qkv_shard = reduce_rows(mm_tn(x, grad_proj).astype(bf16)).astype(f32)

        shard = jnp.concatenate([ffn_shard, qkv_shard, outw_shard], axis=1)
        other = swap(shard, "ctx", 1, n_ctx)
        shard = jnp.concatenate(
            [jnp.where(c == 0, shard, other), jnp.where(c == 0, other, shard)], axis=0
        )
        gated_grad = shard[:, : 2 * hidden].reshape(shard_rows, 2, hidden)
        down_grad = shard[:, 2 * hidden : 3 * hidden]
        qkv_grad = shard[:, 3 * hidden : 3 * hidden + 3 * part].reshape(shard_rows, 3, part)
        outw_grad = shard[:, 3 * hidden + 3 * part :]

        bias_here = jnp.stack(
            [jnp.sum(grad_q.astype(f32), axis=0), jnp.sum(grad_v.astype(f32), axis=0)]
        )
        bias_slot = lax.dynamic_update_slice_in_dim(
            jnp.zeros((2, width), f32), bias_here, t * part, 1
        )
        sums = jnp.concatenate(
            [
                bias_slot,
                jnp.stack(
                    [jnp.sum(grad_pre1, axis=0), ln1g, ln1b, jnp.sum(grad_pre2, axis=0), ln2g, ln2b]
                ),
            ],
            axis=0,
        )
        sums = sum_all(sums, shape)
        qvbias_grad = lax.dynamic_slice_in_dim(sums[:2], t * part, part, 1)
        return (
            layer_output[None],
            input_grad[None],
            qkv_grad,
            qvbias_grad,
            outw_grad,
            sums[2],
            sums[3],
            sums[4],
            gated_grad,
            down_grad,
            sums[5],
            sums[6],
            sums[7],
        )

    return local


def solution(mesh):
    return jax.shard_map(
        make_local(mesh),
        mesh=mesh,
        in_specs=(
            P("wshard", "ctx", None),
            P("wshard"),
            P("wshard", None, "tp"),
            P(None, "tp"),
            P("wshard", "tp"),
            P(),
            P(),
            P(),
            P("wshard", None, "tp"),
            P("wshard", "tp"),
            P(),
            P(),
            P(),
            P("wshard", "ctx", None),
        ),
        out_specs=(
            P("wshard", "ctx", None),
            P("wshard", "ctx", None),
            P("wshard", None, "tp"),
            P(None, "tp"),
            P("wshard", "tp"),
            P(),
            P(),
            P(),
            P("wshard", None, "tp"),
            P("wshard", "tp"),
            P(),
            P(),
            P(),
        ),
        check_vma=False,
    )
```
